768 devices in a mesh: dp: 64 (over y, z_hi, core), tensor: 12 (over z_lo, x).
Axes of the slice: x: 4, y: 8, z: 12 (z_hi: 4, z_lo: 3; z = z_hi * 3 + z_lo), core: 2. Of those that a mesh axis runs over, the one named last changes fastest.
Arguments:
- inputs: bfloat16 [12288, 1536], P('dp'), may hold values from -25 to 25
- w_query: bfloat16 [1536, 3072], P('dp', 'tensor'), may hold values from -1 to 1
- w_keyval: bfloat16 [1536, 1536], P('dp', 'tensor'), may hold values from -1 to 1
- sinks: float32 [48], P('tensor'), may hold values from -1 to 3
- segments: int32 [12288], replicated, may hold values from 0 to 63, never falling along the last dimension, each value on 1 to 384 neighbouring positions
- upstream: bfloat16 [12288, 3072], P('dp', 'tensor'), may hold values from -6 to 6
Outputs:
- attended: bfloat16 [12288, 3072], P('dp', 'tensor')
- grad_inputs: float32 [12288, 1536], P('dp', 'tensor')
- grad_query: float32 [1536, 3072], P('dp', 'tensor')
- grad_keyval: float32 [1536, 1536], P('dp', 'tensor')
The draws below stay inside these ranges and needn't reach their ends.
Inputs may be any that keep to these rules, and one draw needn't show every extreme that they name: `segments`: document numbers never fall along the tokens; each document has at most 384 tokens and one has exactly that many.
All inputs are finite; a program needn't handle non-finite values.
Results may differ from the reference program's by a relative error of at most 0.018.
Values may be sent and summed in bfloat16 or wider, within the bound.
No kernel may reach another device: no remote copies, remote signals or barrier semaphores. Data moves between devices by JAX's collectives and lax.ppermute only.
A program may use at most 32 MiB of HBM per device.

```python
import math
import jax
import jax.numpy as jnp
import numpy as np
from jax import lax

D = 1536
HD = 64
HQ_DEV = 4
WINDOW = 128
TOK_DEV = 192
TOKENS = 12288
KVH = 12
HQ = 48


def weight_parts(key):
    spread_scale = D ** (-0.5)
    shared = jnp.clip(jax.random.normal(jax.random.fold_in(key, 101), (D, KVH, HD), jnp.float32), -6.0, 6.0) * spread_scale
    value_part = jnp.clip(jax.random.normal(jax.random.fold_in(key, 102), (D, KVH, HD), jnp.float32), -6.0, 6.0) * spread_scale
    separate = jnp.clip(jax.random.normal(jax.random.fold_in(key, 103), (D, KVH, HQ_DEV, HD), jnp.float32), -6.0, 6.0) * spread_scale
    return (shared, value_part, separate)


def draw_w_query(key, part):
    shared, value_part, separate = weight_parts(key)
    result = separate
    return result.reshape(D, HQ * HD).astype(jnp.bfloat16)


def draw_w_keyval(key, part):
    shared, value_part, separate = weight_parts(key)
    result = jnp.stack([shared, value_part], axis=2)
    return result.reshape(D, KVH * 2 * HD).astype(jnp.bfloat16)


def draw_inputs(key, part):
    blocks = TOKENS // TOK_DEV
    block_width = D // blocks
    row_index = jnp.arange(TOKENS, dtype=jnp.int32)
    col_index = jnp.arange(D, dtype=jnp.int32)
    pairing = jax.random.permutation(jax.random.fold_in(key, 201), blocks).astype(jnp.int32)
    block_of = row_index // TOK_DEV
    spike_factor = jnp.where(col_index[None, :] // block_width == pairing[block_of][:, None], 4.0, 1.0)
    result = jnp.clip(jax.random.normal(jax.random.fold_in(key, 207), (TOKENS, D), jnp.float32), -6.0, 6.0) * spike_factor
    return result.astype(jnp.bfloat16)


def shard_levels(stream_key, dims, shards, smallest, largest):
    loudness = 1.0
    for position, blocks in shards:
        draws = jax.random.uniform(jax.random.fold_in(jax.random.fold_in(stream_key, 6), position), (blocks,), jnp.float32, smallest / len(shards), largest / len(shards))
        loudness = loudness * jnp.repeat(jnp.exp(draws), dims[position] // blocks).reshape((-1,) + (1,) * (len(dims) - 1 - position))
    return loudness


def split_up(count, total, bound, slope):
    portions = [(1 << 20) // math.isqrt(rank ** slope) + 1 for rank in range(2, count + 1)]
    surplus, given = total - bound - (count - 1), [1] * (count - 1)
    while surplus > 0:
        free = [i for i in range(count - 1) if given[i] < bound]
        whole, budget = sum([portions[i] for i in free]), surplus
        for i in free:
            more = min(bound - given[i], max(1, budget * portions[i] // whole), surplus)
            given[i] = given[i] + more
            surplus = surplus - more
    return np.array([bound] + given)


def ragged_sizes(own_key, amount, total, bound, slope):
    if amount == 2:
        one = jax.random.randint(own_key, (), max(1, total - bound), min(bound, total - 1) + 1)
        return jnp.stack([one, total - one])
    tallies = jnp.asarray(split_up(amount, total, bound, slope), jnp.int32)
    pairs = (amount - 1) // 2
    donor, sink = tallies[1:1 + 2 * pairs:2], tallies[2:2 + 2 * pairs:2]
    slack = jnp.minimum(donor - 1, bound - sink)
    passed = jax.random.randint(jax.random.fold_in(own_key, 1), (pairs,), 0, 1 << 20) % (slack + 1)
    tallies = tallies.at[1:1 + 2 * pairs:2].set(donor - passed).at[2:2 + 2 * pairs:2].set(sink + passed)
    return tallies[jax.random.permutation(jax.random.fold_in(own_key, 2), amount)]


def noise(key, extent, spread, most, split=(), kind=jnp.bfloat16):
    entries = spread * jax.random.normal(key, extent, jnp.float32)
    if split:
        entries = entries * shard_levels(key, extent, split, -0.22, 0.18)
    return jnp.clip(entries, -most, most).astype(kind)


def setup_inputs(seed: int = 0) -> dict:
    key_list = jax.random.split(jax.random.key(seed), 7)
    inputs = draw_inputs(jax.random.fold_in(key_list[6], 71), 0)
    w_query = draw_w_query(jax.random.fold_in(key_list[6], 71), 0)
    w_keyval = draw_w_keyval(jax.random.fold_in(key_list[6], 71), 0)
    sinks = jnp.clip(-1.0 + 4.0 * jax.random.uniform(key_list[3], (HQ,), jnp.float32) ** shard_levels(key_list[3], (HQ,), ((0, 12),), -0.2, 0.2), -1.0, 3.0)
    segments = jnp.searchsorted(jnp.cumsum(ragged_sizes(key_list[4], TOKENS // TOK_DEV, TOKENS, 2 * TOK_DEV, 1)), jnp.arange(TOKENS), side="right").astype(jnp.int32)
    upstream = noise(key_list[5], (TOKENS, HQ * HD), 1.0, 6.0, ((0, 64), (1, 12)))
    return {"inputs": inputs, "w_query": w_query, "w_keyval": w_keyval, "sinks": sinks, "segments": segments, "upstream": upstream}


def attend(query, keys, values, query_seg, key_seg, sinks, upstream):
    count_q = query.shape[0]
    count_k = keys.shape[0]
    scale = HD ** -0.5
    query_f = query.astype(jnp.float32)
    keys_f = keys.astype(jnp.float32)
    values_f = values.astype(jnp.float32)
    upstream_f = upstream.astype(jnp.float32)
    scores = jnp.einsum("qhe,khe->hqk", query_f, keys_f) * scale
    offset = jnp.arange(count_q)[:, None] + WINDOW - jnp.arange(count_k)[None, :]
    allowed = (query_seg[:, None] == key_seg[None, :]) & (offset >= 0) & (offset < WINDOW)
    masked = jnp.where(allowed[None], scores, -1e30)
    top = jnp.maximum(jnp.max(masked, axis=-1), sinks[:, None])
    expo = jnp.where(allowed[None], jnp.exp(masked - top[..., None]), 0.0)
    total = jnp.sum(expo, axis=-1) + jnp.exp(sinks[:, None] - top)
    probs = expo / total[..., None]
    probs_b = probs.astype(jnp.bfloat16).astype(jnp.float32)
    attended = jnp.einsum("hqk,khe->qhe", probs_b, values_f).astype(jnp.bfloat16)
    dprob = jnp.einsum("qhe,khe->hqk", upstream_f, values_f)
    delta = jnp.sum(probs * dprob, axis=-1)
    dscore = (probs * (dprob - delta[..., None])).astype(jnp.bfloat16).astype(jnp.float32)
    grad_q = (jnp.einsum("hqk,khe->qhe", dscore, keys_f) * scale).astype(jnp.bfloat16)
    grad_k = jnp.einsum("hqk,qhe->khe", dscore, query_f) * scale
    grad_v = jnp.einsum("hqk,qhe->khe", probs_b, upstream_f)
    return attended, grad_q, grad_k, grad_v


def reference(inputs, w_query, w_keyval, sinks, segments, upstream):
    query = jnp.dot(inputs, w_query, preferred_element_type=jnp.float32).astype(jnp.bfloat16)
    keyval = jnp.dot(inputs, w_keyval, preferred_element_type=jnp.float32).astype(jnp.bfloat16)
    columns = KVH * 2 * HD
    span = WINDOW + TOK_DEV
    kv_padded = jnp.concatenate([jnp.zeros((WINDOW, columns), jnp.bfloat16), keyval], axis=0)
    seg_padded = jnp.concatenate([jnp.full((WINDOW,), -1, jnp.int32), segments.astype(jnp.int32)], axis=0)

    def one_block(index):
        start = (index * TOK_DEV).astype(jnp.int32)
        block_q = lax.dynamic_slice_in_dim(query, start, TOK_DEV, 0).reshape(TOK_DEV, HQ, HD)
        block_kv = lax.dynamic_slice_in_dim(kv_padded, start, span, 0).reshape(span, KVH, 2, HD)
        keys = jnp.repeat(block_kv[:, :, 0], HQ_DEV, axis=1)
        values = jnp.repeat(block_kv[:, :, 1], HQ_DEV, axis=1)
        query_seg = lax.dynamic_slice_in_dim(segments.astype(jnp.int32), start, TOK_DEV, 0)
        key_seg = lax.dynamic_slice_in_dim(seg_padded, start, span, 0)
        block_up = lax.dynamic_slice_in_dim(upstream, start, TOK_DEV, 0).reshape(TOK_DEV, HQ, HD)
        out_block, grad_q, grad_k, grad_v = attend(block_q, keys, values, query_seg, key_seg, sinks, block_up)
        grad_k = grad_k.reshape(span, KVH, HQ_DEV, HD).sum(axis=2)
        grad_v = grad_v.reshape(span, KVH, HQ_DEV, HD).sum(axis=2)
        grad_kv = jnp.stack([grad_k, grad_v], axis=2).reshape(span, columns)
        return out_block.reshape(TOK_DEV, HQ * HD), grad_q.reshape(TOK_DEV, HQ * HD), grad_kv

    blocks = TOKENS // TOK_DEV
    outs_all, grads_q, grads_kv = lax.map(one_block, jnp.arange(blocks).astype(jnp.int32))
    rims = grads_kv[:, :WINDOW]
    mains = grads_kv[:, WINDOW:]
    incoming = jnp.concatenate([rims[1:], jnp.zeros((1, WINDOW, columns), jnp.float32)], axis=0)
    mains = mains.at[:, TOK_DEV - WINDOW:].add(incoming)
    grad_kv = mains.reshape(TOKENS, columns).astype(jnp.bfloat16)
    attended = outs_all.reshape(TOKENS, HQ * HD)
    grad_q = grads_q.reshape(TOKENS, HQ * HD)
    grad_inputs = jnp.zeros((TOKENS, D), jnp.float32)
    for group_index in range(KVH):
        query_lo = group_index * HQ_DEV * HD
        query_hi = query_lo + HQ_DEV * HD
        keyval_lo = group_index * 2 * HD
        keyval_hi = keyval_lo + 2 * HD
        group_term = jnp.dot(grad_q[:, query_lo:query_hi], w_query[:, query_lo:query_hi].T, preferred_element_type=jnp.float32)
        group_term = group_term + jnp.dot(grad_kv[:, keyval_lo:keyval_hi], w_keyval[:, keyval_lo:keyval_hi].T, preferred_element_type=jnp.float32)
        rounded = lax.optimization_barrier(group_term.astype(jnp.bfloat16))
        grad_inputs = grad_inputs + rounded.astype(jnp.float32)
    grad_query = jnp.dot(inputs.T, grad_q, preferred_element_type=jnp.float32)
    grad_keyval = jnp.dot(inputs.T, grad_kv, preferred_element_type=jnp.float32)
    return attended, grad_inputs, grad_query, grad_keyval
```

```python
import jax
import jax.numpy as jnp
from jax import lax
from jax.sharding import Mesh, PartitionSpec as P

WINDOW = 128
DP = ("y", "zh", "core")
TENSOR = ("zl", "x")
FAR = ("y", "zh")
SWAP = [(0, 1), (1, 0)]


def from_behind(value, axis, steps):
    count = lax.axis_size(axis)
    leading, last = (max(0, -steps), min(count, count - steps))
    return lax.ppermute(value, axis, [(source, source + steps) for source in range(leading, last)])


def exchange(value, axes):
    return lax.all_to_all(value, axes, split_axis=0, concat_axis=0, tiled=True)


def attend(query, keys, values, query_seg, key_seg, sinks, upstream):
    count_q = query.shape[0]
    count_k = keys.shape[0]
    head_dim = keys.shape[1]
    scale = head_dim ** (-0.5)
    scores = jnp.einsum("qhe,ke->hqk", query, keys, preferred_element_type=jnp.float32) * scale
    offset = jnp.arange(count_q)[:, None] + WINDOW - jnp.arange(count_k)[None, :]
    allowed = (query_seg[:, None] == key_seg[None, :]) & (offset >= 0) & (offset < WINDOW)
    masked = jnp.where(allowed[None], scores, -1e30)
    top = jnp.maximum(jnp.max(masked, axis=-1), sinks[:, None])
    expo = jnp.where(allowed[None], jnp.exp(masked - top[..., None]), 0.0)
    total = jnp.sum(expo, axis=-1) + jnp.exp(sinks[:, None] - top)
    probs = expo / total[..., None]
    probs_b = probs.astype(jnp.bfloat16)
    attended = jnp.einsum(
        "hqk,ke->qhe", probs_b, values, preferred_element_type=jnp.float32
    ).astype(jnp.bfloat16)
    dprob = jnp.einsum("qhe,ke->hqk", upstream, values, preferred_element_type=jnp.float32)
    delta = jnp.sum(probs * dprob, axis=-1)
    dscore = (probs * (dprob - delta[..., None])).astype(jnp.bfloat16)
    grad_q = (
        jnp.einsum("hqk,ke->qhe", dscore, keys, preferred_element_type=jnp.float32) * scale
    ).astype(jnp.bfloat16)
    grad_k = jnp.einsum("hqk,qhe->ke", dscore, query, preferred_element_type=jnp.float32) * scale
    grad_v = jnp.einsum("hqk,qhe->ke", probs_b, upstream, preferred_element_type=jnp.float32)
    return (attended, grad_q, jnp.concatenate([grad_k, grad_v], axis=1))


def body(inputs, w_query, w_keyval, sinks, segments, upstream):
    tokens, width = inputs.shape
    head_count = sinks.shape[0]
    head_dim = w_keyval.shape[1] // 2
    split_at = head_count * head_dim
    rows = w_query.shape[0]
    device = lax.axis_index(DP)
    core = lax.axis_index("core")
    far = lax.axis_size(FAR)
    parts = lax.axis_size(TENSOR)

    shard = jnp.concatenate([w_query, w_keyval], axis=1)
    columns = shard.shape[1]
    copies = lax.optimization_barrier(jnp.broadcast_to(shard[None], (far, rows, columns)))
    mine = exchange(copies, FAR)
    other = lax.ppermute(mine, "core", SWAP)
    weights = jnp.stack(
        [jnp.where(core == 0, mine, other), jnp.where(core == 0, other, mine)], axis=1
    ).reshape(width, columns)

    projected = jnp.dot(inputs, weights, preferred_element_type=jnp.float32).astype(jnp.bfloat16)
    query, keyval = projected[:, :split_at], projected[:, split_at:]
    prior = from_behind(keyval[tokens - WINDOW :], DP, 1)
    key_rows = jnp.concatenate([prior, keyval], axis=0)
    seg_padded = jnp.concatenate([jnp.full((WINDOW,), -1, jnp.int32), segments], axis=0)
    query_seg = lax.dynamic_slice_in_dim(seg_padded, device * tokens + WINDOW, tokens, 0)
    key_seg = lax.dynamic_slice_in_dim(seg_padded, device * tokens, tokens + WINDOW, 0)
    heads_q = query.reshape(tokens, head_count, head_dim)
    heads_up = upstream.reshape(tokens, head_count, head_dim)
    attended, grad_q, grad_kv = attend(
        heads_q, key_rows[:, :head_dim], key_rows[:, head_dim:], query_seg, key_seg, sinks, heads_up
    )
    attended = attended.reshape(tokens, split_at)
    grad_q = grad_q.reshape(tokens, split_at)
    owed = from_behind(grad_kv[:WINDOW].astype(jnp.bfloat16), DP, -1).astype(jnp.float32)
    own_kv = grad_kv[WINDOW:] + jnp.concatenate(
        [jnp.zeros((tokens - WINDOW, 2 * head_dim), jnp.float32), owed], axis=0
    )
    combined = jnp.concatenate([grad_q, own_kv.astype(jnp.bfloat16)], axis=1)

    whole_term = lax.dot_general(
        inputs, combined, (((0,), (0,)), ((), ())), preferred_element_type=jnp.float32
    ).astype(jnp.bfloat16).reshape(far, 2, rows, columns)
    theirs = lax.dynamic_index_in_dim(whole_term, 1 - core, 1, keepdims=False)
    ours = lax.dynamic_index_in_dim(whole_term, core, 1, keepdims=False)
    theirs = lax.ppermute(theirs, "core", SWAP)
    pair = (ours.astype(jnp.float32) + theirs.astype(jnp.float32)).astype(jnp.bfloat16)
    grads = jnp.sum(exchange(pair, FAR).astype(jnp.float32), axis=0)

    terms = jnp.einsum(
        "tk,pnk->ptn",
        combined,
        weights.reshape(parts, width // parts, columns),
        preferred_element_type=jnp.float32,
    ).astype(jnp.bfloat16)
    grad_inputs = jnp.sum(exchange(terms, TENSOR).astype(jnp.float32), axis=0)
    return (attended, grad_inputs, grads[:, :split_at], grads[:, split_at:])


def solution(mesh):
    fine = Mesh(mesh.devices.reshape(8, 4, 2, 3, 4), (*DP, *TENSOR))
    return jax.shard_map(
        body,
        mesh=fine,
        in_specs=(
            P(DP, None),
            P(DP, TENSOR),
            P(DP, TENSOR),
            P(TENSOR),
            P(),
            P(DP, TENSOR),
        ),
        out_specs=(P(DP, TENSOR), P(DP, TENSOR), P(DP, TENSOR), P(DP, TENSOR)),
        check_vma=False,
    )
```

```python
import functools

import jax
import jax.numpy as jnp
from jax import lax
from jax.experimental import pallas as pl
from jax.experimental.pallas import tpu as pltpu
from jax.sharding import Mesh, PartitionSpec as P

WINDOW = 128
TILE = 64
DP = ("y", "zh", "core")
TENSOR = ("zl", "x")
FAR = ("y", "zh")
SWAP = [(0, 1), (1, 0)]
F32 = jnp.float32
BF16 = jnp.bfloat16
VMEM = pl.BlockSpec(memory_space=pltpu.VMEM)
SMEM = pl.BlockSpec(memory_space=pltpu.SMEM)


def exchange(value, axes):
    return lax.all_to_all(value, axes, split_axis=0, concat_axis=0, tiled=True)


def project_kernel(core_ref, mine_ref, theirs_ref, w_ref, own_ref, halo_ref, send_ref):
    tokens, columns = own_ref.shape
    kv = columns - 128
    first = core_ref[0] == 0
    mine = jnp.dot(mine_ref[...], w_ref[...], preferred_element_type=F32)
    theirs = jnp.dot(theirs_ref[...], w_ref[...], preferred_element_type=F32)
    own_ref[...] = mine[WINDOW:]
    halo_ref[...] = jnp.where(first, mine[:WINDOW, kv:], theirs[tokens:, kv:])
    send_ref[:, :columns] = theirs[WINDOW:]
    send_ref[: tokens - WINDOW, columns:] = jnp.zeros((tokens - WINDOW, 128), F32)
    send_ref[tokens - WINDOW :, columns:] = jnp.where(first, mine[tokens:, kv:], theirs[:WINDOW, kv:])


def attend_kernel(own_ref, halo_ref, got_ref, up_ref, bias_ref, sinks_ref, att_ref, pack_ref, acc_ref):
    tokens, columns = own_ref.shape
    wide = up_ref.shape[1]
    heads = wide // 64
    proj = own_ref[...] + got_ref[:, :columns]
    halo = halo_ref[...] + got_ref[tokens - WINDOW :, columns:]
    query = (proj[:, :wide].astype(BF16).astype(F32) * 0.125).astype(BF16)
    keyval = jnp.concatenate([halo, proj[:, wide:]], axis=0)
    flipped = jnp.transpose(keyval).astype(BF16)
    keyval = keyval.astype(BF16)
    upstream = up_ref[...]
    sinks = sinks_ref[...]
    acc_ref[...] = jnp.zeros_like(acc_ref)

    def stack(value, start):
        return jnp.concatenate(
            [value[start : start + TILE, 64 * h : 64 * h + 64] for h in range(heads)], axis=0
        )

    for tile in range(tokens // TILE):
        start = tile * TILE
        span = TILE + WINDOW
        qs, us = stack(query, start), stack(upstream, start)
        block = keyval[start : start + span]
        keys, values = block[:, :64], block[:, 64:]
        contract = (((1,), (1,)), ((), ()))
        score = lax.dot_general(keys, qs, contract, preferred_element_type=F32) + bias_ref[tile]
        top = jnp.maximum(jnp.max(score, axis=0, keepdims=True), sinks)
        expo = jnp.exp(score - top)
        total = jnp.sum(expo, axis=0, keepdims=True) + jnp.exp(sinks - top)
        probs = expo * (1.0 / total)
        probs_b = probs.astype(BF16)
        dprob = lax.dot_general(values, us, contract, preferred_element_type=F32)
        delta = jnp.sum(probs * dprob, axis=0, keepdims=True)
        dscore = (probs * (dprob - delta)).astype(BF16)
        part = flipped[:, start : start + span]
        att_t = jnp.dot(part[64:], probs_b, preferred_element_type=F32)
        dq_t = jnp.dot(part[:64], dscore, preferred_element_type=F32) * 0.125
        both = jnp.transpose(jnp.concatenate([att_t, dq_t], axis=0)).astype(BF16)
        for h in range(heads):
            rows = both[h * TILE : (h + 1) * TILE]
            att_ref[start : start + TILE, 64 * h : 64 * h + 64] = rows[:, :64]
            pack_ref[start : start + TILE, 64 * h : 64 * h + 64] = rows[:, 64:]
        grad_k = jnp.dot(dscore, qs, preferred_element_type=F32)
        grad_v = jnp.dot(probs_b, us, preferred_element_type=F32)
        acc_ref[start : start + span] += jnp.concatenate([grad_k, grad_v], axis=1)
    pack_ref[:, wide:columns] = acc_ref[WINDOW:].astype(BF16)
    pack_ref[: tokens - WINDOW, columns:] = jnp.zeros((tokens - WINDOW, 128), BF16)
    pack_ref[tokens - WINDOW :, columns:] = acc_ref[:WINDOW].astype(BF16)


def weight_grad_kernel(core_ref, mine_ref, theirs_ref, pack_ref, got_ref, out_ref, own_ref):
    columns = out_ref.shape[1]
    tokens = pack_ref.shape[0]
    wide = columns - 128
    first = core_ref[0] == 0
    mine_owed = pack_ref[:, columns:]
    theirs_owed = got_ref[:, columns:]
    none = jnp.zeros(mine_owed.shape, F32)
    mine_kv = pack_ref[:, wide:columns].astype(F32) + jnp.where(first, theirs_owed.astype(F32), none)
    theirs_kv = got_ref[:, wide:columns].astype(F32) + jnp.where(first, none, mine_owed.astype(F32))
    mine_kv = mine_kv.astype(BF16)
    own_ref[...] = mine_kv
    zero = jnp.zeros((WINDOW, wide), BF16)
    grads = jnp.concatenate(
        [
            jnp.concatenate([zero, mine_owed[tokens - WINDOW :]], axis=1),
            jnp.concatenate([pack_ref[:, :wide], mine_kv], axis=1),
            jnp.concatenate([zero, theirs_owed[tokens - WINDOW :]], axis=1),
            jnp.concatenate([got_ref[:, :wide], theirs_kv.astype(BF16)], axis=1),
        ],
        axis=0,
    )
    half = WINDOW + tokens
    out_ref[...] = (
        jnp.dot(mine_ref[...], grads[:half], preferred_element_type=F32)
        + jnp.dot(theirs_ref[...], grads[half:], preferred_element_type=F32)
    ).astype(BF16)


def call(kernel, specs, shapes, *args, scratch=()):
    return pl.pallas_call(
        kernel,
        in_specs=specs,
        out_specs=[VMEM] * len(shapes),
        out_shape=[jax.ShapeDtypeStruct(*s) for s in shapes],
        scratch_shapes=scratch,
    )(*args)


def body(inputs, w_query, w_keyval, sinks, segments, upstream):
    tokens, width = inputs.shape
    heads = sinks.shape[0]
    split_at = w_query.shape[1]
    rows = w_query.shape[0]
    columns = split_at + w_keyval.shape[1]
    device = lax.axis_index(DP)
    core = lax.axis_index("core")
    flag = core.reshape(1).astype(jnp.int32)
    count = lax.axis_size(DP)
    far = lax.axis_size(FAR)
    parts = lax.axis_size(TENSOR)
    half = width // 2

    halo = lax.ppermute(inputs[tokens - WINDOW :], DP, [(i - 1, i) for i in range(2, count, 2)])

    shard = jnp.concatenate([w_query, w_keyval], axis=1)
    copies = lax.optimization_barrier(jnp.broadcast_to(shard[None], (far, rows, columns)))
    weights = exchange(copies, FAR).reshape(half, columns)

    source = lax.broadcasted_iota(jnp.int32, (half, 2, half // 2), 0)
    part = lax.broadcasted_iota(jnp.int32, (half, 2, half // 2), 1)
    target = lax.broadcasted_iota(jnp.int32, (half, 2, half // 2), 2)
    chosen = (source == (target // rows) * (2 * rows) + part * rows + target % rows).astype(BF16)
    extended = jnp.concatenate([halo, inputs], axis=0).reshape(WINDOW + tokens, 2, half)
    sorted_x = jnp.einsum("tkd,dhn->htkn", extended, chosen, preferred_element_type=F32).astype(BF16)
    sorted_x = sorted_x.reshape(2, WINDOW + tokens, half)
    mine_x = lax.dynamic_index_in_dim(sorted_x, core, 0, keepdims=False)
    theirs_x = lax.ppermute(
        lax.dynamic_index_in_dim(sorted_x, 1 - core, 0, keepdims=False), "core", SWAP
    )
    mine_xt, theirs_xt = mine_x.T, theirs_x.T

    seg_padded = jnp.concatenate([jnp.full((WINDOW,), -1, jnp.int32), segments], axis=0)
    query_seg = lax.dynamic_slice_in_dim(seg_padded, device * tokens + WINDOW, tokens, 0)
    key_seg = lax.dynamic_slice_in_dim(seg_padded, device * tokens, tokens + WINDOW, 0)
    offset = jnp.arange(TILE)[None, :] + WINDOW - jnp.arange(TILE + WINDOW)[:, None]
    near = (offset >= 0) & (offset < WINDOW)
    bias = jnp.stack(
        [
            jnp.where(
                near
                & (
                    query_seg[None, s : s + TILE] == key_seg[s : s + TILE + WINDOW, None]
                ),
                0.0,
                -1e30,
            )
            for s in range(0, tokens, TILE)
        ]
    ).astype(F32)
    bias = jnp.tile(bias, (1, 1, heads))
    sink_row = jnp.repeat(sinks, TILE)[None, :]

    own, halo_kv, send = call(
        project_kernel,
        [SMEM, VMEM, VMEM, VMEM],
        [((tokens, columns), F32), ((WINDOW, 128), F32), ((tokens, columns + 128), F32)],
        flag,
        mine_x,
        theirs_x,
        weights,
    )
    got = lax.ppermute(send, "core", SWAP)
    attended, pack = call(
        attend_kernel,
        [VMEM] * 6,
        [((tokens, split_at), BF16), ((tokens, columns + 128), BF16)],
        own,
        halo_kv,
        got,
        upstream,
        bias,
        sink_row,
        scratch=[pltpu.VMEM((WINDOW + tokens, 128), F32)],
    )
    got_pack = lax.ppermute(pack, "core", SWAP)
    term, own_kv = call(
        weight_grad_kernel,
        [SMEM] + [VMEM] * 4,
        [((half, columns), BF16), ((tokens, 128), BF16)],
        flag,
        mine_xt,
        theirs_xt,
        pack,
        got_pack,
    )
    received = exchange(term.reshape(far, rows, columns), FAR)
    grad_query = jnp.sum(received[:, :, :split_at].astype(F32), axis=0)
    grad_keyval = jnp.sum(received[:, :, split_at:].astype(F32), axis=0)

    weights, owed, _ = lax.optimization_barrier((weights, pack[tokens - WINDOW :, columns:], term))
    other = lax.ppermute(weights, "core", SWAP)
    owed = lax.ppermute(owed, DP, [(i, i - 1) for i in range(2, count, 2)])
    tail = (own_kv[tokens - WINDOW :].astype(F32) + owed.astype(F32)).astype(BF16)
    own_kv = jnp.concatenate([own_kv[: tokens - WINDOW], tail], axis=0)
    combined = jnp.concatenate([pack[:, :split_at], own_kv], axis=1)
    pair = (weights.reshape(far, rows, columns), other.reshape(far, rows, columns))
    whole = jnp.stack(
        [jnp.where(core == 0, pair[0], pair[1]), jnp.where(core == 0, pair[1], pair[0])], axis=1
    ).reshape(parts, width // parts, columns)
    terms = jnp.einsum("tk,pnk->ptn", combined, whole, preferred_element_type=F32).astype(BF16)
    grad_inputs = jnp.sum(exchange(terms, TENSOR).astype(F32), axis=0)
    return (attended, grad_inputs, grad_query, grad_keyval)


def solution(mesh):
    fine = Mesh(mesh.devices.reshape(8, 4, 2, 3, 4), (*DP, *TENSOR))
    return jax.shard_map(
        body,
        mesh=fine,
        in_specs=(
            P(DP, None),
            P(DP, TENSOR),
            P(DP, TENSOR),
            P(TENSOR),
            P(),
            P(DP, TENSOR),
        ),
        out_specs=(P(DP, TENSOR), P(DP, TENSOR), P(DP, TENSOR), P(DP, TENSOR)),
        check_vma=False,
    )
```

```python
import jax
import jax.numpy as jnp
from jax import lax
from jax.experimental import pallas as pl
from jax.experimental.pallas import tpu as pltpu
from jax.sharding import Mesh, PartitionSpec as P


WINDOW = 128
TILE = 64
DP = ("y", "zh", "core")
TENSOR = ("zl", "x")
FAR = ("zh", "y")
SWAP = [(0, 1), (1, 0)]
F32 = jnp.float32
BF16 = jnp.bfloat16
VMEM = pl.BlockSpec(memory_space=pltpu.VMEM)
SMEM = pl.BlockSpec(memory_space=pltpu.SMEM)


def exchange(value, axes):
    return lax.all_to_all(value, axes, split_axis=0, concat_axis=0, tiled=True)


def spread(blocks, axis):
    size, here = blocks.shape[0], lax.axis_index(axis)
    got = [lax.dynamic_index_in_dim(blocks, here, 0, keepdims=False)]
    for step in range(1, size):
        block = lax.dynamic_index_in_dim(blocks, (here + step) % size, 0, keepdims=False)
        got.append(lax.ppermute(block, axis, [(i, (i + step) % size) for i in range(size)]))
    return sum(block.astype(F32) for block in got)


def project_kernel(core_ref, mine_ref, theirs_ref, w_ref, own_ref, halo_ref, send_ref):
    tokens, columns = own_ref.shape
    kv = columns - 128
    first = core_ref[0] == 0
    mine = jnp.dot(mine_ref[...], w_ref[...], preferred_element_type=F32)
    theirs = jnp.dot(theirs_ref[...], w_ref[...], preferred_element_type=F32)
    own_ref[...] = mine[WINDOW:]
    halo_ref[...] = jnp.where(first, mine[:WINDOW, kv:], theirs[tokens:, kv:])
    send_ref[:, :columns] = theirs[WINDOW:]
    send_ref[: tokens - WINDOW, columns:] = jnp.zeros((tokens - WINDOW, 128), F32)
    send_ref[tokens - WINDOW :, columns:] = jnp.where(first, mine[tokens:, kv:], theirs[:WINDOW, kv:])


def attend_kernel(own_ref, halo_ref, got_ref, up_ref, bias_ref, sinks_ref, att_ref, pack_ref, acc_ref):
    tokens, columns = own_ref.shape
    wide = up_ref.shape[1]
    heads = wide // 64
    proj = own_ref[...] + got_ref[:, :columns]
    halo = halo_ref[...] + got_ref[tokens - WINDOW :, columns:]
    query = (proj[:, :wide].astype(BF16).astype(F32) * 0.125).astype(BF16)
    keyval = jnp.concatenate([halo, proj[:, wide:]], axis=0)
    flipped = jnp.transpose(keyval).astype(BF16)
    keyval = keyval.astype(BF16)
    upstream = up_ref[...]
    sinks = sinks_ref[...]
    acc_ref[...] = jnp.zeros_like(acc_ref)

    def stack(value, start):
        return jnp.concatenate(
            [value[start : start + TILE, 64 * h : 64 * h + 64] for h in range(heads)], axis=0
        )

    for tile in range(tokens // TILE):
        start = tile * TILE
        span = TILE + WINDOW
        qs, us = stack(query, start), stack(upstream, start)
        block = keyval[start : start + span]
        keys, values = block[:, :64], block[:, 64:]
        contract = (((1,), (1,)), ((), ()))
        score = lax.dot_general(keys, qs, contract, preferred_element_type=F32) + bias_ref[tile]
        top = jnp.maximum(jnp.max(score, axis=0, keepdims=True), sinks)
        expo = jnp.exp(score - top)
        total = jnp.sum(expo, axis=0, keepdims=True) + jnp.exp(sinks - top)
        probs = expo * (1.0 / total)
        probs_b = probs.astype(BF16)
        dprob = lax.dot_general(values, us, contract, preferred_element_type=F32)
        delta = jnp.sum(probs * dprob, axis=0, keepdims=True)
        dscore = (probs * (dprob - delta)).astype(BF16)
        part = flipped[:, start : start + span]
        att_t = jnp.dot(part[64:], probs_b, preferred_element_type=F32)
        dq_t = jnp.dot(part[:64], dscore, preferred_element_type=F32) * 0.125
        both = jnp.transpose(jnp.concatenate([att_t, dq_t], axis=0)).astype(BF16)
        for h in range(heads):
            rows = both[h * TILE : (h + 1) * TILE]
            att_ref[start : start + TILE, 64 * h : 64 * h + 64] = rows[:, :64]
            pack_ref[start : start + TILE, 64 * h : 64 * h + 64] = rows[:, 64:]
        grad_k = jnp.dot(dscore, qs, preferred_element_type=F32)
        grad_v = jnp.dot(probs_b, us, preferred_element_type=F32)
        acc_ref[start : start + span] += jnp.concatenate([grad_k, grad_v], axis=1)
    pack_ref[:, wide:columns] = acc_ref[WINDOW:].astype(BF16)
    pack_ref[: tokens - WINDOW, columns:] = jnp.zeros((tokens - WINDOW, 128), BF16)
    pack_ref[tokens - WINDOW :, columns:] = acc_ref[:WINDOW].astype(BF16)


def weight_grad_kernel(core_ref, mine_ref, theirs_ref, pack_ref, got_ref, out_ref, own_ref):
    columns = out_ref.shape[1]
    tokens = pack_ref.shape[0]
    wide = columns - 128
    first = core_ref[0] == 0
    mine_owed = pack_ref[:, columns:]
    theirs_owed = got_ref[:, columns:]
    none = jnp.zeros(mine_owed.shape, F32)
    mine_kv = pack_ref[:, wide:columns].astype(F32) + jnp.where(first, theirs_owed.astype(F32), none)
    theirs_kv = got_ref[:, wide:columns].astype(F32) + jnp.where(first, none, mine_owed.astype(F32))
    mine_kv = mine_kv.astype(BF16)
    own_ref[...] = mine_kv
    zero = jnp.zeros((WINDOW, wide), BF16)
    grads = jnp.concatenate(
        [
            jnp.concatenate([zero, mine_owed[tokens - WINDOW :]], axis=1),
            jnp.concatenate([pack_ref[:, :wide], mine_kv], axis=1),
            jnp.concatenate([zero, theirs_owed[tokens - WINDOW :]], axis=1),
            jnp.concatenate([got_ref[:, :wide], theirs_kv.astype(BF16)], axis=1),
        ],
        axis=0,
    )
    half = WINDOW + tokens
    out_ref[...] = (
        jnp.dot(mine_ref[...], grads[:half], preferred_element_type=F32)
        + jnp.dot(theirs_ref[...], grads[half:], preferred_element_type=F32)
    ).astype(BF16)


def call(kernel, specs, shapes, *args, scratch=()):
    placed = [
        a if s is SMEM else pltpu.with_memory_space_constraint(a, pltpu.VMEM)
        for a, s in zip(args, specs)
    ]
    return pl.pallas_call(
        kernel,
        in_specs=specs,
        out_specs=[VMEM] * len(shapes),
        out_shape=[pltpu.VMEM(*s) for s in shapes],
        scratch_shapes=scratch,
    )(*placed)


def body(inputs, w_query, w_keyval, sinks, segments, upstream):
    tokens, width = inputs.shape
    heads = sinks.shape[0]
    split_at = w_query.shape[1]
    rows = w_query.shape[0]
    columns = split_at + w_keyval.shape[1]
    device = lax.axis_index(DP)
    core = lax.axis_index("core")
    flag = core.reshape(1).astype(jnp.int32)
    count = lax.axis_size(DP)
    far = lax.axis_size(FAR)
    parts = lax.axis_size(TENSOR)
    half = width // 2

    halo = lax.ppermute(
        inputs[tokens - WINDOW :], DP, [(i - 1, i) for i in range(2, count, 2)]
    )

    shard = jnp.concatenate([w_query, w_keyval], axis=1)
    copies = lax.optimization_barrier(jnp.broadcast_to(shard[None], (far, rows, columns)))
    weights = exchange(copies, FAR).reshape(half, columns)

    near, outer = lax.axis_size(FAR[1]), lax.axis_size(FAR[0])
    target = jnp.arange(width, dtype=jnp.int32)
    block = target % half // rows
    wanted = ((block % near * outer + block // near) * 2 + target // half) * rows + target % rows
    chosen = (jnp.arange(width, dtype=jnp.int32)[:, None] == wanted[None, :]).astype(BF16)
    extended = jnp.concatenate([halo, inputs], axis=0)
    sorted_x = jnp.dot(extended, chosen, preferred_element_type=F32).astype(BF16)
    mine_x = jnp.where(core == 0, sorted_x[:, :half], sorted_x[:, half:])
    theirs_x = jnp.where(core == 0, sorted_x[:, half:], sorted_x[:, :half])
    theirs_x = lax.ppermute(theirs_x, "core", SWAP)
    mine_xt, theirs_xt = mine_x.T, theirs_x.T

    seg_padded = jnp.concatenate([jnp.full((WINDOW,), -1, jnp.int32), segments], axis=0)
    query_seg = lax.dynamic_slice_in_dim(seg_padded, device * tokens + WINDOW, tokens, 0)
    key_seg = lax.dynamic_slice_in_dim(seg_padded, device * tokens, tokens + WINDOW, 0)
    offset = jnp.arange(TILE)[None, :] + WINDOW - jnp.arange(TILE + WINDOW)[:, None]
    reach = (offset >= 0) & (offset < WINDOW)
    bias = jnp.stack(
        [
            jnp.where(
                reach
                & (
                    query_seg[None, s : s + TILE] == key_seg[s : s + TILE + WINDOW, None]
                ),
                0.0,
                -1e30,
            )
            for s in range(0, tokens, TILE)
        ]
    ).astype(F32)
    bias = jnp.tile(bias, (1, 1, heads))
    sink_row = jnp.repeat(sinks, TILE)[None, :]

    weights, mine_xt, theirs_xt, bias, sink_row = lax.optimization_barrier(
        (weights, mine_xt, theirs_xt, bias, sink_row)
    )
    own, halo_kv, send = call(
        project_kernel,
        [SMEM, VMEM, VMEM, VMEM],
        [((tokens, columns), F32), ((WINDOW, 128), F32), ((tokens, columns + 128), F32)],
        flag,
        mine_x,
        theirs_x,
        weights,
    )
    got = lax.ppermute(send, "core", SWAP)
    other = lax.ppermute(weights, "core", SWAP)
    attended, pack = call(
        attend_kernel,
        [VMEM] * 6,
        [((tokens, split_at), BF16), ((tokens, columns + 128), BF16)],
        own,
        halo_kv,
        got,
        upstream,
        bias,
        sink_row,
        scratch=[pltpu.VMEM((WINDOW + tokens, 128), F32)],
    )
    got_pack = lax.ppermute(pack, "core", SWAP)
    owed = lax.ppermute(
        pack[tokens - WINDOW :, columns:], DP, [(i, i - 1) for i in range(2, count, 2)]
    )
    term, own_kv = call(
        weight_grad_kernel,
        [SMEM] + [VMEM] * 4,
        [((half, columns), BF16), ((tokens, 128), BF16)],
        flag,
        mine_xt,
        theirs_xt,
        pack,
        got_pack,
    )
    received = exchange(term.reshape(far, rows, columns), FAR)
    grad_query = jnp.sum(received[:, :, :split_at].astype(F32), axis=0)
    grad_keyval = jnp.sum(received[:, :, split_at:].astype(F32), axis=0)

    tail = (own_kv[tokens - WINDOW :].astype(F32) + owed.astype(F32)).astype(BF16)
    own_kv = jnp.concatenate([own_kv[: tokens - WINDOW], tail], axis=0)
    combined = jnp.concatenate([pack[:, :split_at], own_kv], axis=1)
    weights, other, combined, _ = lax.optimization_barrier((weights, other, combined, term))
    pair = (weights.reshape(far, rows, columns), other.reshape(far, rows, columns))
    whole = jnp.stack(
        [jnp.where(core == 0, pair[0], pair[1]), jnp.where(core == 0, pair[1], pair[0])], axis=1
    ).reshape(outer, near, 2 * rows, columns)
    deep, across = (lax.axis_size(axis) for axis in TENSOR)
    whole = jnp.swapaxes(whole, 0, 1).reshape(deep, across, width // parts, columns)
    terms = jnp.einsum("tk,zxck->xtzc", combined, whole, preferred_element_type=F32).astype(BF16)
    terms = terms.reshape(across, tokens, width // across)
    near_sum = spread(terms, "x")
    near_sum = jnp.swapaxes(near_sum.astype(BF16).reshape(tokens, deep, width // parts), 0, 1)
    grad_inputs = spread(near_sum, "zl")
    return (attended, grad_inputs, grad_query, grad_keyval)


def solution(mesh):
    fine = Mesh(mesh.devices.reshape(8, 4, 2, 3, 4), (*DP, *TENSOR))

    return jax.shard_map(
        body,
        mesh=fine,
        in_specs=(
            P(DP, None),
            P(DP, TENSOR),
            P(DP, TENSOR),
            P(TENSOR),
            P(),
            P(DP, TENSOR),
        ),
        out_specs=(P(DP, TENSOR), P(DP, TENSOR), P(DP, TENSOR), P(DP, TENSOR)),
        check_vma=False,
    )
```

```python
import jax
import jax.numpy as jnp
from jax import lax
from jax.experimental import pallas as pl
from jax.experimental.pallas import tpu as pltpu
from jax.sharding import Mesh, PartitionSpec as P


WINDOW = 128
TILE = 64
DP = ("y", "zh", "core")
TENSOR = ("zl", "x")
FAR = ("zh", "y")
SWAP = [(0, 1), (1, 0)]
F32 = jnp.float32
BF16 = jnp.bfloat16
VMEM = pl.BlockSpec(memory_space=pltpu.VMEM)
SMEM = pl.BlockSpec(memory_space=pltpu.SMEM)


def exchange(value, axes):
    return lax.all_to_all(value, axes, split_axis=0, concat_axis=0, tiled=True)


def dot(a, b):
    return jnp.dot(a, b, preferred_element_type=F32)


def mask_kernel(query_ref, key_ref, bias_ref):
    tiles, span, lanes = bias_ref.shape
    key = lax.broadcasted_iota(jnp.int32, (span, TILE), 0)
    offset = lax.broadcasted_iota(jnp.int32, (span, TILE), 1) + WINDOW - key
    reach = (offset >= 0) & (offset < WINDOW)
    for tile in range(tiles):
        start = tile * TILE
        same = query_ref[:, start : start + TILE] == key_ref[start : start + span, :]
        bias = jnp.where(reach & same, 0.0, -1e30).astype(F32)
        bias_ref[tile] = jnp.concatenate([bias] * (lanes // TILE), axis=1)


def project_kernel(core_ref, mine_ref, theirs_ref, w_ref, edge_ref, keep_ref, send_ref):
    tokens, wide = send_ref.shape
    columns = wide - 128
    first = core_ref[0] == 0
    theirs = dot(theirs_ref[...], w_ref[...])
    mine_kv = dot(mine_ref[...], w_ref[:, columns - 128 :])
    send_ref[:, :columns] = theirs
    send_ref[:, columns:] = mine_kv
    theirs_last = theirs[tokens - WINDOW :, columns - 128 :]
    edge_ref[...] = jnp.where(first, theirs_last, mine_kv[tokens - WINDOW :])
    keep_ref[...] = theirs_last


def attend_kernel(
    core_ref, mine_ref, w_ref, got_ref, keep_ref, even_ref, odd_ref, up_ref, bias_ref, sinks_ref,
    att_ref, pack_ref, acc_ref,
):
    tokens, wide = up_ref.shape
    columns = w_ref.shape[1]
    heads = wide // 64
    proj = dot(mine_ref[...], w_ref[...]) + got_ref[:, :columns]
    halo = jnp.where(
        core_ref[0] == 0,
        even_ref[...] + odd_ref[...],
        keep_ref[...] + got_ref[tokens - WINDOW :, columns:],
    )
    query = (proj[:, :wide].astype(BF16).astype(F32) * 0.125).astype(BF16)
    keyval = jnp.concatenate([halo, proj[:, wide:]], axis=0)
    flipped = jnp.transpose(keyval).astype(BF16)
    keyval = keyval.astype(BF16)
    upstream = up_ref[...]
    sinks = sinks_ref[...]
    acc_ref[...] = jnp.zeros_like(acc_ref)

    def stack(value, start):
        return jnp.concatenate(
            [value[start : start + TILE, 64 * h : 64 * h + 64] for h in range(heads)], axis=0
        )

    for tile in range(tokens // TILE):
        start = tile * TILE
        span = TILE + WINDOW
        qs, us = stack(query, start), stack(upstream, start)
        block = keyval[start : start + span]
        keys, values = block[:, :64], block[:, 64:]
        contract = (((1,), (1,)), ((), ()))
        score = lax.dot_general(keys, qs, contract, preferred_element_type=F32) + bias_ref[tile]
        top = jnp.maximum(jnp.max(score, axis=0, keepdims=True), sinks)
        expo = jnp.exp(score - top)
        total = jnp.sum(expo, axis=0, keepdims=True) + jnp.exp(sinks - top)
        probs = expo * (1.0 / total)
        probs_b = probs.astype(BF16)
        dprob = lax.dot_general(values, us, contract, preferred_element_type=F32)
        delta = jnp.sum(probs * dprob, axis=0, keepdims=True)
        dscore = (probs * (dprob - delta)).astype(BF16)
        part = flipped[:, start : start + span]
        att_t = dot(part[64:], probs_b)
        dq_t = dot(part[:64], dscore) * 0.125
        both = jnp.transpose(jnp.concatenate([att_t, dq_t], axis=0)).astype(BF16)
        for h in range(heads):
            rows = both[h * TILE : (h + 1) * TILE]
            att_ref[start : start + TILE, 64 * h : 64 * h + 64] = rows[:, :64]
            pack_ref[start : start + TILE, 64 * h : 64 * h + 64] = rows[:, 64:]
        grads = jnp.concatenate([dot(dscore, qs), dot(probs_b, us)], axis=1)
        acc_ref[start : start + span] += grads
    pack_ref[:, wide:columns] = acc_ref[WINDOW:].astype(BF16)
    pack_ref[: tokens - WINDOW, columns:] = jnp.zeros((tokens - WINDOW, 128), BF16)
    pack_ref[tokens - WINDOW :, columns:] = acc_ref[:WINDOW].astype(BF16)


def weight_grad_kernel(
    place_ref, mine_ref, theirs_ref, pack_ref, got_ref, even_ref, odd_ref, whole_ref,
    out_ref, term_ref,
):
    columns = out_ref.shape[1]
    tokens = pack_ref.shape[0]
    wide = columns - 128
    across, deep = term_ref.shape[0], term_ref.shape[2] // 128
    first = place_ref[0] == 0
    here = place_ref[1]
    none = jnp.zeros((tokens, 128), F32)
    late = even_ref[...].astype(F32) + odd_ref[...].astype(F32)
    late = jnp.concatenate([none[: tokens - WINDOW], late], axis=0)
    mine_kv = pack_ref[:, wide:columns].astype(F32) + jnp.where(
        first, got_ref[:, columns:].astype(F32), late
    )
    theirs_kv = got_ref[:, wide:columns].astype(F32) + jnp.where(
        first, late, pack_ref[:, columns:].astype(F32)
    )
    mine = jnp.concatenate([pack_ref[:, :wide], mine_kv.astype(BF16)], axis=1)
    theirs = jnp.concatenate([got_ref[:, :wide], theirs_kv.astype(BF16)], axis=1)
    for x in range(across):
        slot = (x + across - here) % across
        for z in range(deep):
            rows = whole_ref[128 * (z * across + x) : 128 * (z * across + x + 1), :]
            block = lax.dot_general(
                mine, rows, (((1,), (1,)), ((), ())), preferred_element_type=F32
            )
            term_ref[slot, :, 128 * z : 128 * z + 128] = block.astype(BF16)
    out_ref[...] = (dot(mine_ref[...], mine) + dot(theirs_ref[...], theirs)).astype(BF16)


def call(kernel, specs, shapes, *args, scratch=()):
    placed = [
        a if s is SMEM else pltpu.with_memory_space_constraint(a, pltpu.VMEM)
        for a, s in zip(args, specs)
    ]
    return pl.pallas_call(
        kernel,
        in_specs=specs,
        out_specs=[VMEM] * len(shapes),
        out_shape=[pltpu.VMEM(*s) for s in shapes],
        scratch_shapes=scratch,
        compiler_params=pltpu.CompilerParams(vmem_limit_bytes=16 << 20),
    )(*placed)


def body(inputs, w_query, w_keyval, sinks, segments, upstream):
    tokens, width = inputs.shape
    heads = sinks.shape[0]
    split_at = w_query.shape[1]
    rows = w_query.shape[0]
    columns = split_at + w_keyval.shape[1]
    device = lax.axis_index(DP)
    core = lax.axis_index("core")
    place = jnp.stack([core, lax.axis_index("x")]).astype(jnp.int32)
    count = lax.axis_size(DP)
    far = lax.axis_size(FAR)
    outer, near = (lax.axis_size(axis) for axis in FAR)
    deep, across = (lax.axis_size(axis) for axis in TENSOR)
    half = width // 2
    span = TILE + WINDOW

    shard = jnp.concatenate([w_query, w_keyval], axis=1)
    copies = lax.optimization_barrier(jnp.broadcast_to(shard[None], (far, rows, columns)))
    weights = exchange(copies, FAR).reshape(half, columns)

    target = jnp.arange(width, dtype=jnp.int32)
    block = target % half // rows
    wanted = ((block % near * outer + block // near) * 2 + target // half) * rows + target % rows
    chosen = (jnp.arange(width, dtype=jnp.int32)[:, None] == wanted[None, :]).astype(BF16)
    sorted_x = dot(inputs, chosen).astype(BF16)
    mine_x = jnp.where(core == 0, sorted_x[:, :half], sorted_x[:, half:])
    theirs_x = jnp.where(core == 0, sorted_x[:, half:], sorted_x[:, :half])
    theirs_x = lax.ppermute(theirs_x, "core", SWAP)
    mine_xt, theirs_xt = mine_x.T, theirs_x.T

    seg_padded = jnp.concatenate([jnp.full((WINDOW,), -1, jnp.int32), segments], axis=0)
    query_seg = lax.dynamic_slice_in_dim(seg_padded, device * tokens + WINDOW, tokens, 0)
    key_seg = lax.dynamic_slice_in_dim(seg_padded, device * tokens, tokens + WINDOW, 0)
    (bias,) = call(
        mask_kernel,
        [VMEM] * 2,
        [((tokens // TILE, span, heads * TILE), F32)],
        query_seg[None, :],
        key_seg[:, None],
    )
    sink_row = jnp.repeat(sinks, TILE)[None, :]

    weights, mine_xt, theirs_xt, bias, sink_row, upstream = lax.optimization_barrier(
        (weights, mine_xt, theirs_xt, bias, sink_row, upstream)
    )
    edge, keep, send = call(
        project_kernel,
        [SMEM] + [VMEM] * 3,
        [((WINDOW, 128), F32), ((WINDOW, 128), F32), ((tokens, columns + 128), F32)],
        place,
        mine_x,
        theirs_x,
        weights,
    )
    even = lax.ppermute(edge, DP, [(i, i + 2) for i in range(0, count - 2, 2)])
    odd = lax.ppermute(edge, DP, [(i, i + 1) for i in range(1, count - 2, 2)])
    got = lax.ppermute(send, "core", SWAP)
    other = lax.ppermute(weights, "core", SWAP)
    attended, pack = call(
        attend_kernel,
        [SMEM] + [VMEM] * 9,
        [((tokens, split_at), BF16), ((tokens, columns + 128), BF16)],
        place,
        mine_x,
        weights,
        got,
        keep,
        even,
        odd,
        upstream,
        bias,
        sink_row,
        scratch=[pltpu.VMEM((WINDOW + tokens, 128), F32)],
    )
    owed = pack[tokens - WINDOW :, columns:]
    even = lax.ppermute(owed, DP, [(i, i - 2) for i in range(2, count, 2)])
    odd = lax.ppermute(owed, DP, [(i, i - 1) for i in range(2, count, 2)])
    got_pack = lax.ppermute(pack, "core", SWAP)

    pair = (weights.reshape(far, rows, columns), other.reshape(far, rows, columns))
    whole = jnp.stack(
        [jnp.where(core == 0, pair[0], pair[1]), jnp.where(core == 0, pair[1], pair[0])], axis=1
    ).reshape(outer, near, 2 * rows, columns)
    whole = jnp.swapaxes(whole, 0, 1).reshape(width, columns)

    term, blocks = call(
        weight_grad_kernel,
        [SMEM] + [VMEM] * 7,
        [((half, columns), BF16), ((across, tokens, width // across), BF16)],
        place,
        mine_xt,
        theirs_xt,
        pack,
        got_pack,
        even,
        odd,
        whole,
    )
    got_x = [
        lax.ppermute(blocks[s], "x", [(i, (i + s) % across) for i in range(across)])
        for s in range(1, across)
    ]
    received = exchange(term.reshape(far, rows, columns), FAR)
    sums = sum((g.astype(F32) for g in got_x), blocks[0].astype(F32)).astype(BF16)
    sums = [sums[:, 128 * z : 128 * z + 128] for z in range(deep)]
    depth = lax.axis_index("zl")

    def pick(step):
        return lax.select_n((depth + step) % deep, *sums)

    got_z = [
        lax.ppermute(pick(s), "zl", [(i, (i + s) % deep) for i in range(deep)])
        for s in range(1, deep)
    ]
    grad_inputs = sum((g.astype(F32) for g in got_z), pick(0).astype(F32))
    grad_query = jnp.sum(received[:, :, :split_at].astype(F32), axis=0)
    grad_keyval = jnp.sum(received[:, :, split_at:].astype(F32), axis=0)
    return (attended, grad_inputs, grad_query, grad_keyval)


def solution(mesh):
    fine = Mesh(mesh.devices.reshape(8, 4, 2, 3, 4), (*DP, *TENSOR))

    return jax.shard_map(
        body,
        mesh=fine,
        in_specs=(
            P(DP, None),
            P(DP, TENSOR),
            P(DP, TENSOR),
            P(TENSOR),
            P(),
            P(DP, TENSOR),
        ),
        out_specs=(P(DP, TENSOR), P(DP, TENSOR), P(DP, TENSOR), P(DP, TENSOR)),
        check_vma=False,
    )
```

```python
import jax
import jax.numpy as jnp
from jax import lax
from jax.experimental import pallas as pl
from jax.experimental.pallas import tpu as pltpu
from jax.sharding import Mesh, PartitionSpec as P


WINDOW = 128
TILE = 64
DP = ("y", "zh", "core")
TENSOR = ("zl", "x")
SWAP = [(0, 1), (1, 0)]
F32 = jnp.float32
BF16 = jnp.bfloat16
VMEM = pl.BlockSpec(memory_space=pltpu.VMEM)
SMEM = pl.BlockSpec(memory_space=pltpu.SMEM)


def exchange(value, axes):
    return lax.all_to_all(value, axes, split_axis=0, concat_axis=0, tiled=True)


def dot(a, b):
    return jnp.dot(a, b, preferred_element_type=F32)


def mask_kernel(query_ref, key_ref, bias_ref):
    tiles, span, lanes = bias_ref.shape
    key = lax.broadcasted_iota(jnp.int32, (span, TILE), 0)
    offset = lax.broadcasted_iota(jnp.int32, (span, TILE), 1) + WINDOW - key
    reach = (offset >= 0) & (offset < WINDOW)
    for tile in range(tiles):
        start = tile * TILE
        same = query_ref[:, start : start + TILE] == key_ref[start : start + span, :]
        bias = jnp.where(reach & same, 0.0, -1e30).astype(F32)
        bias_ref[tile] = jnp.concatenate([bias] * (lanes // TILE), axis=1)


def sort_kernel(wanted_ref, x_ref, mine_ref, theirs_ref, chosen_ref):
    half = wanted_ref.shape[1]
    source = lax.broadcasted_iota(jnp.int32, (half, half), 0)
    chosen_ref[...] = jnp.where(source == wanted_ref[...], 1.0, 0.0).astype(BF16)
    split(chosen_ref, x_ref, mine_ref, theirs_ref)


def resort_kernel(chosen_ref, x_ref, mine_ref, theirs_ref):
    split(chosen_ref, x_ref, mine_ref, theirs_ref)


def split(chosen_ref, x_ref, mine_ref, theirs_ref):
    half = chosen_ref.shape[1]
    for part in range(x_ref.shape[1] // half):
        both = dot(x_ref[:, part * half : (part + 1) * half], chosen_ref[...]).astype(BF16)
        columns = slice(part * half // 2, (part + 1) * half // 2)
        mine_ref[:, columns] = both[:, : half // 2]
        theirs_ref[:, columns] = both[:, half // 2 :]


def flip_kernel(
    core_ref, mine_ref, theirs_ref, halo_ref, other_ref, out_ref, mine_t_ref, theirs_t_ref, halo_t_ref
):
    @pl.when(core_ref[0] == 0)
    def _():
        out_ref[...] = halo_ref[...]

    @pl.when(core_ref[0] != 0)
    def _():
        out_ref[...] = other_ref[...]

    mine_t_ref[...] = jnp.transpose(mine_ref[...])
    theirs_t_ref[...] = jnp.transpose(theirs_ref[...])
    halo_t_ref[...] = jnp.transpose(out_ref[...])


def project_kernel(core_ref, mine_ref, theirs_ref, halo_ref, w_ref, keep_ref, send_ref):
    tokens, wide = send_ref.shape
    columns = wide - 128
    first = core_ref[0] == 0
    theirs = dot(theirs_ref[...], w_ref[...])
    mine_kv = dot(mine_ref[...], w_ref[:, columns - 128 :])
    halo_kv = dot(halo_ref[...], w_ref[:, columns - 128 :])
    send_ref[:, :columns] = theirs
    send_ref[: tokens - WINDOW, columns:] = mine_kv[: tokens - WINDOW]
    send_ref[tokens - WINDOW :, columns:] = jnp.where(first, mine_kv[tokens - WINDOW :], halo_kv)
    keep_ref[...] = jnp.where(first, halo_kv, theirs[tokens - WINDOW :, columns - 128 :])


def attend_kernel(
    mine_ref, w_ref, got_ref, keep_ref, up_ref, bias_ref, sinks_ref, att_ref, pack_ref, acc_ref
):
    tokens, wide = up_ref.shape
    columns = w_ref.shape[1]
    heads = wide // 64
    proj = dot(mine_ref[...], w_ref[...]) + got_ref[:, :columns]
    halo = keep_ref[...] + got_ref[tokens - WINDOW :, columns:]
    query = (proj[:, :wide].astype(BF16).astype(F32) * 0.125).astype(BF16)
    keyval = jnp.concatenate([halo, proj[:, wide:]], axis=0)
    flipped = jnp.transpose(keyval).astype(BF16)
    keyval = keyval.astype(BF16)
    upstream = up_ref[...]
    sinks = sinks_ref[...]
    acc_ref[...] = jnp.zeros_like(acc_ref)

    def stack(value, start):
        return jnp.concatenate(
            [value[start : start + TILE, 64 * h : 64 * h + 64] for h in range(heads)], axis=0
        )

    for tile in range(tokens // TILE):
        start = tile * TILE
        span = TILE + WINDOW
        qs, us = stack(query, start), stack(upstream, start)
        block = keyval[start : start + span]
        keys, values = block[:, :64], block[:, 64:]
        contract = (((1,), (1,)), ((), ()))
        score = lax.dot_general(keys, qs, contract, preferred_element_type=F32) + bias_ref[tile]
        top = jnp.maximum(jnp.max(score, axis=0, keepdims=True), sinks)
        expo = jnp.exp(score - top)
        total = jnp.sum(expo, axis=0, keepdims=True) + jnp.exp(sinks - top)
        probs = expo * (1.0 / total)
        probs_b = probs.astype(BF16)
        dprob = lax.dot_general(values, us, contract, preferred_element_type=F32)
        delta = jnp.sum(probs * dprob, axis=0, keepdims=True)
        dscore = (probs * (dprob - delta)).astype(BF16)
        part = flipped[:, start : start + span]
        att_t = dot(part[64:], probs_b)
        dq_t = dot(part[:64], dscore) * 0.125
        both = jnp.transpose(jnp.concatenate([att_t, dq_t], axis=0)).astype(BF16)
        for h in range(heads):
            rows = both[h * TILE : (h + 1) * TILE]
            att_ref[start : start + TILE, 64 * h : 64 * h + 64] = rows[:, :64]
            pack_ref[start : start + TILE, 64 * h : 64 * h + 64] = rows[:, 64:]
        grads = jnp.concatenate([dot(dscore, qs), dot(probs_b, us)], axis=1)
        acc_ref[start : start + span] += grads
    pack_ref[:, wide:columns] = acc_ref[WINDOW:].astype(BF16)
    pack_ref[: tokens - WINDOW, columns:] = jnp.zeros((tokens - WINDOW, 128), BF16)
    pack_ref[tokens - WINDOW :, columns:] = acc_ref[:WINDOW].astype(BF16)


def weight_grad_kernel(core_ref, mine_ref, theirs_ref, halo_ref, pack_ref, got_ref, out_ref, own_ref):
    columns = out_ref.shape[1]
    tokens = pack_ref.shape[0]
    wide = columns - 128
    first = core_ref[0] == 0
    mine_owed, theirs_owed = pack_ref[:, columns:], got_ref[:, columns:]
    none = jnp.zeros((tokens, 128), F32)
    mine_kv = pack_ref[:, wide:columns].astype(F32) + jnp.where(first, theirs_owed.astype(F32), none)
    theirs_kv = got_ref[:, wide:columns].astype(F32) + jnp.where(first, none, mine_owed.astype(F32))
    mine_kv = mine_kv.astype(BF16)
    own_ref[...] = mine_kv
    owed = jnp.where(first, mine_owed.astype(F32), theirs_owed.astype(F32)).astype(BF16)
    out_ref[:, :wide] = (
        dot(mine_ref[...], pack_ref[:, :wide]) + dot(theirs_ref[...], got_ref[:, :wide])
    ).astype(BF16)
    out_ref[:, wide:] = (
        dot(mine_ref[...], mine_kv)
        + dot(theirs_ref[...], theirs_kv.astype(BF16))
        + dot(halo_ref[...], owed[tokens - WINDOW :])
    ).astype(BF16)


def input_grad_kernel(place_ref, pack_ref, own_ref, late_ref, w_ref, other_ref, term_ref, whole_ref):
    tokens = pack_ref.shape[0]
    wide = whole_ref.shape[1] - 128
    across, deep = term_ref.shape[0], term_ref.shape[2] // 128
    here = place_ref[1]
    rows = 24

    def interleave(first_ref, second_ref):
        for start in range(0, w_ref.shape[0], rows):
            whole_ref[2 * start : 2 * start + rows] = first_ref[start : start + rows]
            whole_ref[2 * start + rows : 2 * start + 2 * rows] = second_ref[start : start + rows]

    pl.when(place_ref[0] == 0)(lambda: interleave(w_ref, other_ref))
    pl.when(place_ref[0] != 0)(lambda: interleave(other_ref, w_ref))
    tail = own_ref[tokens - WINDOW :].astype(F32) + late_ref[...].astype(F32)
    keyval = jnp.concatenate([own_ref[: tokens - WINDOW], tail.astype(BF16)], axis=0)
    mine = jnp.concatenate([pack_ref[:, :wide], keyval], axis=1)
    for x in range(across):
        slot = (x + across - here) % across
        for z in range(deep):
            rows = whole_ref[128 * (z * across + x) : 128 * (z * across + x + 1), :]
            block = lax.dot_general(
                mine, rows, (((1,), (1,)), ((), ())), preferred_element_type=F32
            )
            term_ref[slot, :, 128 * z : 128 * z + 128] = block.astype(BF16)


def near_sum_kernel(depth_ref, blocks_ref, *refs):
    *got_refs, out_ref = refs
    total = blocks_ref[0].astype(F32)
    for got in got_refs:
        total += got[...].astype(F32)
    deep = out_ref.shape[0]
    for z in range(deep):
        slot = (z + deep - depth_ref[0]) % deep
        out_ref[slot] = total[:, 128 * z : 128 * z + 128].astype(BF16)


def last_sum_kernel(grads_ref, sums_ref, *refs):
    *got_refs, inputs_ref, query_ref, keyval_ref = refs
    total = sums_ref[0].astype(F32)
    for got in got_refs:
        total += got[...].astype(F32)
    inputs_ref[...] = total
    grads = grads_ref[0].astype(F32)
    for index in range(1, grads_ref.shape[0]):
        grads += grads_ref[index].astype(F32)
    wide = query_ref.shape[1]
    query_ref[...] = grads[:, :wide]
    keyval_ref[...] = grads[:, wide:]


def call(kernel, specs, shapes, *args, scratch=()):
    placed = [
        a if s is SMEM else pltpu.with_memory_space_constraint(a, pltpu.VMEM)
        for a, s in zip(args, specs)
    ]
    return pl.pallas_call(
        kernel,
        in_specs=specs,
        out_specs=[VMEM] * len(shapes),
        out_shape=[pltpu.VMEM(*s) for s in shapes],
        scratch_shapes=scratch,
        compiler_params=pltpu.CompilerParams(vmem_limit_bytes=16 << 20),
    )(*placed)


def body(inputs, w_query, w_keyval, sinks, segments, upstream):
    tokens, width = inputs.shape
    heads = sinks.shape[0]
    split_at = w_query.shape[1]
    rows = w_query.shape[0]
    columns = split_at + w_keyval.shape[1]
    device = lax.axis_index(DP)
    core = lax.axis_index("core")
    flag = core.reshape(1).astype(jnp.int32)
    place = jnp.stack([core, lax.axis_index("x")]).astype(jnp.int32)
    depth = lax.axis_index("zl").reshape(1).astype(jnp.int32)
    count = lax.axis_size(DP)
    outer, near = lax.axis_size("y"), lax.axis_size("zh")
    deep, across = (lax.axis_size(axis) for axis in TENSOR)
    half = width // 2
    span = TILE + WINDOW

    shard = jnp.concatenate([w_query, w_keyval], axis=1)
    copies = lax.optimization_barrier(jnp.broadcast_to(shard[None], (near, rows, columns)))
    weights = exchange(copies, "zh")
    weights = weights.reshape(1, near * rows, columns)
    copies = lax.optimization_barrier(
        jnp.broadcast_to(weights, (outer, near * rows, columns))
    )
    weights = exchange(copies, "y").reshape(half, columns)

    target = jnp.arange(half, dtype=jnp.int32)
    part = jnp.where(target < half // 2, core, 1 - core)
    wanted = (target % (half // 2) // rows * 2 + part) * rows + target % rows
    halo = lax.ppermute(
        inputs[tokens - WINDOW :], DP, [(i - 1, i) for i in range(2, count, 2)]
    )
    mine_x, theirs_x, chosen = call(
        sort_kernel,
        [VMEM] * 2,
        [((tokens, half), BF16), ((tokens, half), BF16), ((half, half), BF16)],
        wanted[None, :],
        inputs,
    )
    theirs_x = lax.ppermute(theirs_x, "core", SWAP)
    halo, other_halo = call(
        resort_kernel,
        [VMEM] * 2,
        [((WINDOW, half), BF16), ((WINDOW, half), BF16)],
        chosen,
        halo,
    )
    other_halo = lax.ppermute(other_halo, "core", [(0, 1)])
    halo, mine_xt, theirs_xt, halo_t = call(
        flip_kernel,
        [SMEM] + [VMEM] * 4,
        [
            ((WINDOW, half), BF16),
            ((half, tokens), BF16),
            ((half, tokens), BF16),
            ((half, WINDOW), BF16),
        ],
        flag,
        mine_x,
        theirs_x,
        halo,
        other_halo,
    )

    seg_padded = jnp.concatenate([jnp.full((WINDOW,), -1, jnp.int32), segments], axis=0)
    query_seg = lax.dynamic_slice_in_dim(seg_padded, device * tokens + WINDOW, tokens, 0)
    key_seg = lax.dynamic_slice_in_dim(seg_padded, device * tokens, tokens + WINDOW, 0)
    (bias,) = call(
        mask_kernel,
        [VMEM] * 2,
        [((tokens // TILE, span, heads * TILE), F32)],
        query_seg[None, :],
        key_seg[:, None],
    )
    sink_row = jnp.repeat(sinks, TILE)[None, :]

    weights, mine_xt, theirs_xt, halo_t, bias, sink_row, upstream = lax.optimization_barrier(
        (weights, mine_xt, theirs_xt, halo_t, bias, sink_row, upstream)
    )
    keep, send = call(
        project_kernel,
        [SMEM] + [VMEM] * 4,
        [((WINDOW, 128), F32), ((tokens, columns + 128), F32)],
        flag,
        mine_x,
        theirs_x,
        halo,
        weights,
    )
    got = lax.ppermute(send, "core", SWAP)
    other = lax.ppermute(weights, "core", SWAP)
    attended, pack = call(
        attend_kernel,
        [VMEM] * 7,
        [((tokens, split_at), BF16), ((tokens, columns + 128), BF16)],
        mine_x,
        weights,
        got,
        keep,
        upstream,
        bias,
        sink_row,
        scratch=[pltpu.VMEM((WINDOW + tokens, 128), F32)],
    )
    got_pack = lax.ppermute(pack, "core", SWAP)
    late = lax.ppermute(
        pack[tokens - WINDOW :, columns:], DP, [(i, i - 1) for i in range(2, count, 2)]
    )

    term, own_kv = call(
        weight_grad_kernel,
        [SMEM] + [VMEM] * 5,
        [((half, columns), BF16), ((tokens, 128), BF16)],
        flag,
        mine_xt,
        theirs_xt,
        halo_t,
        pack,
        got_pack,
    )
    (blocks,) = call(
        input_grad_kernel,
        [SMEM] + [VMEM] * 5,
        [((across, tokens, width // across), BF16)],
        place,
        pack,
        own_kv,
        late,
        weights,
        other,
        scratch=[pltpu.VMEM((width, columns), BF16)],
    )
    term = exchange(term.reshape(outer, near * rows, columns), "y")
    term = jnp.sum(term.astype(F32), axis=0).astype(BF16)
    received = exchange(term.reshape(near, rows, columns), "zh")
    got_x = [
        lax.ppermute(blocks[s], "x", [(i, (i + s) % across) for i in range(across)])
        for s in range(1, across)
    ]
    (sums,) = call(
        near_sum_kernel,
        [SMEM] + [VMEM] * across,
        [((deep, tokens, 128), BF16)],
        depth,
        blocks,
        *got_x,
    )
    got_z = [
        lax.ppermute(sums[s], "zl", [(i, (i + s) % deep) for i in range(deep)])
        for s in range(1, deep)
    ]
    grad_inputs, grad_query, grad_keyval = pl.pallas_call(
        last_sum_kernel,
        in_specs=[VMEM] * (deep + 1),
        out_specs=[VMEM] * 3,
        out_shape=[
            jax.ShapeDtypeStruct((tokens, 128), F32),
            jax.ShapeDtypeStruct((rows, split_at), F32),
            jax.ShapeDtypeStruct((rows, columns - split_at), F32),
        ],
        compiler_params=pltpu.CompilerParams(vmem_limit_bytes=16 << 20),
    )(*(pltpu.with_memory_space_constraint(a, pltpu.VMEM) for a in (received, sums, *got_z)))
    return (attended, grad_inputs, grad_query, grad_keyval)


def solution(mesh):
    fine = Mesh(mesh.devices.reshape(8, 4, 2, 3, 4), (*DP, *TENSOR))

    return jax.shard_map(
        body,
        mesh=fine,
        in_specs=(
            P(DP, None),
            P(DP, TENSOR),
            P(DP, TENSOR),
            P(TENSOR),
            P(),
            P(DP, TENSOR),
        ),
        out_specs=(P(DP, TENSOR), P(DP, TENSOR), P(DP, TENSOR), P(DP, TENSOR)),
        check_vma=False,
    )
```

```python
import jax
import jax.numpy as jnp
from jax import lax
from jax.experimental import pallas as pl
from jax.experimental.pallas import tpu as pltpu
from jax.sharding import Mesh, PartitionSpec as P


WINDOW = 128
TILE = 64
DP = ("y", "zh", "core")
TENSOR = ("zl", "x")
SWAP = [(0, 1), (1, 0)]
F32 = jnp.float32
BF16 = jnp.bfloat16
VMEM = pl.BlockSpec(memory_space=pltpu.VMEM)
FETCH = pl.BlockSpec(memory_space=pltpu.VMEM)
SMEM = pl.BlockSpec(memory_space=pltpu.SMEM)


def groups_of(sizes, axis):
    outer, near, cores = sizes
    count = sizes[axis]
    groups = []
    for rest in range(outer * near // count):
        for core in range(cores):
            members = [(rank + core * count // 2) % count for rank in range(count)]
            chips = [m * near + rest if axis == 0 else rest * near + m for m in members]
            groups.append([chip * cores + core for chip in chips])
    return groups


def exchange(value, axis):
    sizes = [lax.axis_size(name) for name in DP]
    groups = groups_of(sizes, DP.index(axis))
    return lax.all_to_all(
        value, DP, split_axis=0, concat_axis=0, tiled=True, axis_index_groups=groups
    )


def dot(a, b):
    return jnp.dot(a, b, preferred_element_type=F32)


def mask_kernel(query_ref, key_ref, up_ref, bias_ref, held_ref):
    held_ref[...] = up_ref[...]
    tiles, span, lanes = bias_ref.shape
    key = lax.broadcasted_iota(jnp.int32, (span, TILE), 0)
    offset = lax.broadcasted_iota(jnp.int32, (span, TILE), 1) + WINDOW - key
    reach = (offset >= 0) & (offset < WINDOW)
    for tile in range(tiles):
        start = tile * TILE
        same = query_ref[:, start : start + TILE] == key_ref[start : start + span, :]
        bias = jnp.where(reach & same, 0.0, -1e30).astype(F32)
        bias_ref[tile] = jnp.concatenate([bias] * (lanes // TILE), axis=1)


def sort_kernel(core_ref, wanted_ref, x_ref, mine_ref, theirs_ref, chosen_ref):
    half = wanted_ref.shape[1]
    source = lax.broadcasted_iota(jnp.int32, (half, half), 0)
    chosen_ref[...] = jnp.where(source == wanted_ref[...], 1.0, 0.0).astype(BF16)
    split(core_ref, chosen_ref, x_ref, mine_ref, theirs_ref)


def resort_kernel(core_ref, chosen_ref, x_ref, mine_ref, theirs_ref):
    split(core_ref, chosen_ref, x_ref, mine_ref, theirs_ref)


def split(core_ref, chosen_ref, x_ref, mine_ref, theirs_ref):
    half = chosen_ref.shape[1]
    wide = half // 2
    for part in range(2):
        both = dot(x_ref[:, part * half : (part + 1) * half], chosen_ref[...]).astype(BF16)
        plain = slice(part * wide, (part + 1) * wide)
        turned = slice((1 - part) * wide, (2 - part) * wide)

        @pl.when(core_ref[0] == 0)
        def _():
            mine_ref[:, plain] = both[:, :wide]
            theirs_ref[:, turned] = both[:, wide:]

        @pl.when(core_ref[0] != 0)
        def _():
            mine_ref[:, turned] = both[:, :wide]
            theirs_ref[:, plain] = both[:, wide:]


def flip_kernel(
    core_ref, mine_ref, theirs_ref, halo_ref, other_ref, out_ref, mine_t_ref, theirs_t_ref, halo_t_ref
):
    @pl.when(core_ref[0] == 0)
    def _():
        out_ref[...] = halo_ref[...]

    @pl.when(core_ref[0] != 0)
    def _():
        out_ref[...] = other_ref[...]

    mine_t_ref[...] = jnp.transpose(mine_ref[...])
    theirs_t_ref[...] = jnp.transpose(theirs_ref[...])
    halo_t_ref[...] = jnp.transpose(out_ref[...])


def project_kernel(core_ref, mine_ref, theirs_ref, halo_ref, w_ref, keep_ref, send_ref):
    tokens, wide = send_ref.shape
    columns = wide - 128
    first = core_ref[0] == 0
    theirs = dot(theirs_ref[...], w_ref[...])
    mine_kv = dot(mine_ref[...], w_ref[:, columns - 128 :])
    halo_kv = dot(halo_ref[...], w_ref[:, columns - 128 :])
    send_ref[:, :columns] = theirs
    send_ref[: tokens - WINDOW, columns:] = mine_kv[: tokens - WINDOW]
    send_ref[tokens - WINDOW :, columns:] = jnp.where(first, mine_kv[tokens - WINDOW :], halo_kv)
    keep_ref[...] = jnp.where(first, halo_kv, theirs[tokens - WINDOW :, columns - 128 :])


def attend_kernel(
    mine_ref, w_ref, got_ref, keep_ref, up_ref, bias_ref, sinks_ref, att_ref, pack_ref, acc_ref
):
    tokens, wide = up_ref.shape
    columns = w_ref.shape[1]
    heads = wide // 64
    proj = dot(mine_ref[...], w_ref[...]) + got_ref[:, :columns]
    halo = keep_ref[...] + got_ref[tokens - WINDOW :, columns:]
    query = (proj[:, :wide].astype(BF16).astype(F32) * 0.125).astype(BF16)
    keyval = jnp.concatenate([halo, proj[:, wide:]], axis=0)
    flipped = jnp.transpose(keyval).astype(BF16)
    keyval = keyval.astype(BF16)
    upstream = up_ref[...]
    sinks = sinks_ref[...]
    acc_ref[...] = jnp.zeros_like(acc_ref)

    def stack(value, start):
        return jnp.concatenate(
            [value[start : start + TILE, 64 * h : 64 * h + 64] for h in range(heads)], axis=0
        )

    for tile in range(tokens // TILE):
        start = tile * TILE
        span = TILE + WINDOW
        qs, us = stack(query, start), stack(upstream, start)
        block = keyval[start : start + span]
        keys, values = block[:, :64], block[:, 64:]
        contract = (((1,), (1,)), ((), ()))
        score = lax.dot_general(keys, qs, contract, preferred_element_type=F32) + bias_ref[tile]
        top = jnp.maximum(jnp.max(score, axis=0, keepdims=True), sinks)
        expo = jnp.exp(score - top)
        total = jnp.sum(expo, axis=0, keepdims=True) + jnp.exp(sinks - top)
        probs = expo * (1.0 / total)
        probs_b = probs.astype(BF16)
        dprob = lax.dot_general(values, us, contract, preferred_element_type=F32)
        delta = jnp.sum(probs * dprob, axis=0, keepdims=True)
        dscore = (probs * (dprob - delta)).astype(BF16)
        part = flipped[:, start : start + span]
        att_t = dot(part[64:], probs_b)
        dq_t = dot(part[:64], dscore) * 0.125
        both = jnp.transpose(jnp.concatenate([att_t, dq_t], axis=0)).astype(BF16)
        for h in range(heads):
            rows = both[h * TILE : (h + 1) * TILE]
            att_ref[start : start + TILE, 64 * h : 64 * h + 64] = rows[:, :64]
            pack_ref[start : start + TILE, 64 * h : 64 * h + 64] = rows[:, 64:]
        grads = jnp.concatenate([dot(dscore, qs), dot(probs_b, us)], axis=1)
        acc_ref[start : start + span] += grads
    pack_ref[:, wide:columns] = acc_ref[WINDOW:].astype(BF16)
    pack_ref[: tokens - WINDOW, columns:] = jnp.zeros((tokens - WINDOW, 128), BF16)
    pack_ref[tokens - WINDOW :, columns:] = acc_ref[:WINDOW].astype(BF16)


def weight_grad_kernel(core_ref, mine_ref, theirs_ref, halo_ref, pack_ref, got_ref, out_ref, own_ref):
    columns = out_ref.shape[1]
    tokens = pack_ref.shape[0]
    wide = columns - 128
    first = core_ref[0] == 0
    mine_owed, theirs_owed = pack_ref[:, columns:], got_ref[:, columns:]
    none = jnp.zeros((tokens, 128), F32)
    mine_kv = pack_ref[:, wide:columns].astype(F32) + jnp.where(first, theirs_owed.astype(F32), none)
    theirs_kv = got_ref[:, wide:columns].astype(F32) + jnp.where(first, none, mine_owed.astype(F32))
    mine_kv = mine_kv.astype(BF16)
    own_ref[...] = mine_kv
    owed = jnp.where(first, mine_owed.astype(F32), theirs_owed.astype(F32)).astype(BF16)
    out_ref[:, :wide] = (
        dot(mine_ref[...], pack_ref[:, :wide]) + dot(theirs_ref[...], got_ref[:, :wide])
    ).astype(BF16)
    out_ref[:, wide:] = (
        dot(mine_ref[...], mine_kv)
        + dot(theirs_ref[...], theirs_kv.astype(BF16))
        + dot(halo_ref[...], owed[tokens - WINDOW :])
    ).astype(BF16)


def input_grad_kernel(place_ref, pack_ref, own_ref, late_ref, w_ref, other_ref, term_ref, whole_ref):
    tokens = pack_ref.shape[0]
    wide = whole_ref.shape[1] - 128
    across, deep = term_ref.shape[0], term_ref.shape[2] // 128
    here = place_ref[1]
    rows = 24

    def interleave(first_ref, second_ref):
        blocks = w_ref.shape[0] // rows
        for index in range(blocks):
            into = 2 * index * rows
            y, z = index // 4, index % 4
            turned = (((y + blocks // 8) % (blocks // 4)) * 4 + (z + 2) % 4) * rows
            whole_ref[into : into + rows] = first_ref[index * rows : (index + 1) * rows]
            whole_ref[into + rows : into + 2 * rows] = second_ref[turned : turned + rows]

    pl.when(place_ref[0] == 0)(lambda: interleave(w_ref, other_ref))
    pl.when(place_ref[0] != 0)(lambda: interleave(other_ref, w_ref))
    tail = own_ref[tokens - WINDOW :].astype(F32) + late_ref[...].astype(F32)
    keyval = jnp.concatenate([own_ref[: tokens - WINDOW], tail.astype(BF16)], axis=0)
    mine = jnp.concatenate([pack_ref[:, :wide], keyval], axis=1)
    for x in range(across):
        slot = (x + across - here) % across
        for z in range(deep):
            rows = whole_ref[128 * (z * across + x) : 128 * (z * across + x + 1), :]
            block = lax.dot_general(
                mine, rows, (((1,), (1,)), ((), ())), preferred_element_type=F32
            )
            term_ref[slot, :, 128 * z : 128 * z + 128] = block.astype(BF16)


def near_sum_kernel(depth_ref, blocks_ref, *refs):
    *got_refs, out_ref = refs
    total = blocks_ref[0].astype(F32)
    for got in got_refs:
        total += got[...].astype(F32)
    deep = out_ref.shape[0]
    for z in range(deep):
        slot = (z + deep - depth_ref[0]) % deep
        out_ref[slot] = total[:, 128 * z : 128 * z + 128].astype(BF16)


def last_sum_kernel(grads_ref, sums_ref, *refs):
    *got_refs, inputs_ref, query_ref, keyval_ref = refs
    total = sums_ref[0].astype(F32)
    for got in got_refs:
        total += got[...].astype(F32)
    inputs_ref[...] = total
    grads = grads_ref[0].astype(F32)
    for index in range(1, grads_ref.shape[0]):
        grads += grads_ref[index].astype(F32)
    wide = query_ref.shape[1]
    query_ref[...] = grads[:, :wide]
    keyval_ref[...] = grads[:, wide:]


def call(kernel, specs, shapes, *args, scratch=()):
    placed = [
        pltpu.with_memory_space_constraint(a, pltpu.VMEM) if s is VMEM else a
        for a, s in zip(args, specs)
    ]
    return pl.pallas_call(
        kernel,
        in_specs=specs,
        out_specs=[VMEM] * len(shapes),
        out_shape=[pltpu.VMEM(*s) for s in shapes],
        scratch_shapes=scratch,
        compiler_params=pltpu.CompilerParams(vmem_limit_bytes=16 << 20),
    )(*placed)


def body(inputs, w_query, w_keyval, sinks, segments, upstream):
    tokens, width = inputs.shape
    heads = sinks.shape[0]
    split_at = w_query.shape[1]
    rows = w_query.shape[0]
    columns = split_at + w_keyval.shape[1]
    device = lax.axis_index(DP)
    core = lax.axis_index("core")
    flag = core.reshape(1).astype(jnp.int32)
    place = jnp.stack([core, lax.axis_index("x")]).astype(jnp.int32)
    depth = lax.axis_index("zl").reshape(1).astype(jnp.int32)
    count = lax.axis_size(DP)
    outer, near = lax.axis_size("y"), lax.axis_size("zh")
    deep, across = (lax.axis_size(axis) for axis in TENSOR)
    half = width // 2
    span = TILE + WINDOW

    shard = jnp.concatenate([w_query, w_keyval], axis=1)
    copies = lax.optimization_barrier(jnp.broadcast_to(shard[None], (near, rows, columns)))
    weights = exchange(copies, "zh")
    weights = weights.reshape(1, near * rows, columns)
    copies = lax.optimization_barrier(
        jnp.broadcast_to(weights, (outer, near * rows, columns))
    )
    weights = exchange(copies, "y").reshape(half, columns)

    target = jnp.arange(half, dtype=jnp.int32)
    part = jnp.where(target < half // 2, core, 1 - core)
    block = target % (half // 2) // rows
    block = block // near * near + (block % near + part * (near // 2)) % near
    wanted = (block * 2 + part) * rows + target % rows
    halo = lax.ppermute(
        inputs[tokens - WINDOW :], DP, [(i - 1, i) for i in range(2, count, 2)]
    )
    mine_x, theirs_x, chosen = call(
        sort_kernel,
        [SMEM] + [VMEM] * 2,
        [((tokens, half), BF16), ((tokens, half), BF16), ((half, half), BF16)],
        flag,
        wanted[None, :],
        inputs,
    )
    theirs_x = lax.ppermute(theirs_x, "core", SWAP)
    halo, other_halo = call(
        resort_kernel,
        [SMEM] + [VMEM] * 2,
        [((WINDOW, half), BF16), ((WINDOW, half), BF16)],
        flag,
        chosen,
        halo,
    )
    other_halo = lax.ppermute(other_halo, "core", [(0, 1)])
    halo, mine_xt, theirs_xt, halo_t = call(
        flip_kernel,
        [SMEM] + [VMEM] * 3 + [FETCH],
        [
            ((WINDOW, half), BF16),
            ((half, tokens), BF16),
            ((half, tokens), BF16),
            ((half, WINDOW), BF16),
        ],
        flag,
        mine_x,
        theirs_x,
        halo,
        other_halo,
    )

    seg_padded = jnp.concatenate([jnp.full((WINDOW,), -1, jnp.int32), segments], axis=0)
    query_seg = lax.dynamic_slice_in_dim(seg_padded, device * tokens + WINDOW, tokens, 0)
    key_seg = lax.dynamic_slice_in_dim(seg_padded, device * tokens, tokens + WINDOW, 0)
    bias, upstream = call(
        mask_kernel,
        [VMEM] * 2 + [FETCH],
        [((tokens // TILE, span, heads * TILE), F32), (upstream.shape, BF16)],
        query_seg[None, :],
        key_seg[:, None],
        upstream,
    )
    sink_row = jnp.repeat(sinks, TILE)[None, :]

    weights, mine_xt, theirs_xt, halo_t, bias, sink_row, upstream = lax.optimization_barrier(
        (weights, mine_xt, theirs_xt, halo_t, bias, sink_row, upstream)
    )
    keep, send = call(
        project_kernel,
        [SMEM] + [VMEM] * 4,
        [((WINDOW, 128), F32), ((tokens, columns + 128), F32)],
        flag,
        mine_x,
        theirs_x,
        halo,
        weights,
    )
    got = lax.ppermute(send, "core", SWAP)
    other = lax.ppermute(weights, "core", SWAP)
    attended, pack = call(
        attend_kernel,
        [VMEM] * 7,
        [((tokens, split_at), BF16), ((tokens, columns + 128), BF16)],
        mine_x,
        weights,
        got,
        keep,
        upstream,
        bias,
        sink_row,
        scratch=[pltpu.VMEM((WINDOW + tokens, 128), F32)],
    )
    got_pack = lax.ppermute(pack, "core", SWAP)
    late = lax.ppermute(
        pack[tokens - WINDOW :, columns:], DP, [(i, i - 1) for i in range(2, count, 2)]
    )

    term, own_kv = call(
        weight_grad_kernel,
        [SMEM] + [VMEM] * 5,
        [((half, columns), BF16), ((tokens, 128), BF16)],
        flag,
        mine_xt,
        theirs_xt,
        halo_t,
        pack,
        got_pack,
    )
    (blocks,) = call(
        input_grad_kernel,
        [SMEM] + [VMEM] * 5,
        [((across, tokens, width // across), BF16)],
        place,
        pack,
        own_kv,
        late,
        weights,
        other,
        scratch=[pltpu.VMEM((width, columns), BF16)],
    )
    term = exchange(term.reshape(outer, near * rows, columns), "y")
    term = jnp.sum(term.astype(F32), axis=0).astype(BF16)
    received = exchange(term.reshape(near, rows, columns), "zh")
    got_x = [
        lax.ppermute(blocks[s], "x", [(i, (i + s) % across) for i in range(across)])
        for s in range(1, across)
    ]
    (sums,) = call(
        near_sum_kernel,
        [SMEM] + [VMEM] * across,
        [((deep, tokens, 128), BF16)],
        depth,
        blocks,
        *got_x,
    )
    got_z = [
        lax.ppermute(sums[s], "zl", [(i, (i + s) % deep) for i in range(deep)])
        for s in range(1, deep)
    ]
    grad_inputs, grad_query, grad_keyval = pl.pallas_call(
        last_sum_kernel,
        in_specs=[VMEM] * (deep + 1),
        out_specs=[VMEM] * 3,
        out_shape=[
            jax.ShapeDtypeStruct((tokens, 128), F32),
            jax.ShapeDtypeStruct((rows, split_at), F32),
            jax.ShapeDtypeStruct((rows, columns - split_at), F32),
        ],
        compiler_params=pltpu.CompilerParams(vmem_limit_bytes=16 << 20),
    )(*(pltpu.with_memory_space_constraint(a, pltpu.VMEM) for a in (received, sums, *got_z)))
    return (attended, grad_inputs, grad_query, grad_keyval)


def solution(mesh):
    fine = Mesh(mesh.devices.reshape(8, 4, 2, 3, 4), (*DP, *TENSOR))

    return jax.shard_map(
        body,
        mesh=fine,
        in_specs=(
            P(DP, None),
            P(DP, TENSOR),
            P(DP, TENSOR),
            P(TENSOR),
            P(),
            P(DP, TENSOR),
        ),
        out_specs=(P(DP, TENSOR), P(DP, TENSOR), P(DP, TENSOR), P(DP, TENSOR)),
        check_vma=False,
    )
```
